256 devices in a mesh: dp: 16 (over x_lo, z), expert: 16 (over y, x_hi, core).
Axes of the slice: x: 4 (x_hi: 2, x_lo: 2; x = x_hi * 2 + x_lo), y: 4, z: 8, core: 2. Of those that a mesh axis runs over, the one named last changes fastest.
Arguments:
- out_grad: bfloat16 [32768, 4096], P(('dp', 'expert')), may hold values from -6 to 6
- expert_ids: int32 [32768, 4], P(('dp', 'expert')), may hold values from 0 to 15, all different within a row; in each aligned block of 128 rows (0 to 127, 128 to 255, ...) at most 48 rows name the same one
- gate_weights: bfloat16 [32768, 4], P(('dp', 'expert')), may hold values from 0.019897461 to 0.5
- saved_acts: bfloat16 [16, 16, 16, 48, 1536], P('dp', None, 'expert'), may hold values from -8 to 8
- down_weight: bfloat16 [16, 4096, 768], P('expert', 'dp'), may hold values from -0.09375 to 0.09375
Outputs:
- pre_grads: bfloat16 [16, 16, 16, 48, 1536], P('dp', None, 'expert')
- down_grad: bfloat16 [16, 4096, 768], P('expert', 'dp')
- gate_grad: float32 [32768, 4], P(('dp', 'expert'))
The draws below stay inside these ranges and needn't reach their ends.
Inputs may be any that keep to these rules, and one draw needn't show every extreme that they name: `expert_ids`: each token names 4 different experts; among the 128 tokens of one device no expert is named by more than 48 tokens, a bound that some block reaches.
All inputs are finite; a program needn't handle non-finite values.
Results may differ from the reference program's by a relative error of at most 0.0057.
Values may be sent and summed in bfloat16 or wider, within the bound.
A program may use at most 192 MiB of HBM per device.

```python
import math
import jax
import jax.numpy as jnp
import numpy as np
from jax import lax

D = 4096
FF_W = 768
TOPK = 4
EXPERTS = 16
TOK_DEV = 128
CAP = 48
TOKENS = 32768
N_DP = 16
N_EXPERT = 16


def levels(own_key, extent, cuts, low, high):
    def one(axis_at, shards_of):
        draws = jax.random.uniform(jax.random.fold_in(jax.random.fold_in(own_key, 6), axis_at), (shards_of,), jnp.float32, low / len(cuts), high / len(cuts))
        return jnp.repeat(jnp.exp(draws), extent[axis_at] // shards_of).reshape((-1,) + (1,) * (len(extent) - axis_at - 1))

    loudness = one(*cuts[0])
    for cut in cuts[1:]:
        loudness = loudness * one(*cut)
    return loudness


def shared_out(key, own, number, rows, amount, top, limit, lean):
    order = jax.random.permutation(key, amount)
    crowded, ordinary = shares(amount, rows * top, limit, lean, True), shares(amount, rows * top, limit, lean, False)
    places = jnp.arange(amount)

    def named(tallies, offset_by):
        used = int((tallies > 0).sum())
        fixed = max(1, used // 4)
        shifted = fixed + (places - fixed + offset_by * (used - fixed)) % max(1, amount - fixed)
        return jnp.zeros((amount,), jnp.int32).at[order[jnp.where(places < fixed, places, shifted)]].set(jnp.asarray(tallies, jnp.int32))

    tallies = jnp.where(number % 4 == 0, named(crowded, number // 4), named(ordinary, number - number // 4 - 1))
    mixed = jax.random.permutation(jax.random.fold_in(own, 3), amount)
    source_of, taker = mixed[0:amount // 2 * 2:2], mixed[1:amount // 2 * 2:2]
    margin = jnp.minimum(tallies[source_of] - 1, limit - tallies[taker]) // 2
    margin = jnp.where((source_of == order[0]) | (taker == order[0]) | (tallies[taker] == 0), 0, jnp.maximum(margin, 0))
    shifted = jax.random.randint(jax.random.fold_in(own, 4), (amount // 2,), 0, 1 << 20) % (margin + 1)
    tallies = tallies.at[source_of].add(-shifted).at[taker].add(shifted)
    items = jnp.searchsorted(jnp.cumsum(tallies), jnp.arange(rows * top), side="right").astype(jnp.int32)
    listing = items.reshape(top, rows).T
    listing = listing[jax.random.permutation(jax.random.fold_in(own, 1), rows)]
    offset_by = jax.random.randint(jax.random.fold_in(own, 2), (rows, 1), 0, top)
    return jnp.take_along_axis(listing, (jnp.arange(top)[None, :] + offset_by) % top, axis=1)


def shares(number_of, total, reach, skew, full):
    loads = [(1 << 20) // math.isqrt(standing ** skew) + 1 for standing in range(1, number_of + 1)]
    largest = reach if full else min(reach, max(-(-total // number_of), total * loads[0] // sum(loads)))
    least = 1 if total - largest >= number_of - 1 else 0
    counts, rest = [largest] + [least] * (number_of - 1), total - largest - least * (number_of - 1)
    while rest > 0:
        candidates = [i for i in range(1, number_of) if counts[i] < largest] or [i for i in range(1, number_of) if counts[i] < reach]
        pool, left = sum([loads[i] for i in candidates]), rest
        for i in candidates:
            extra = min(reach - counts[i], max(1, left * loads[i] // pool), rest)
            counts[i] = counts[i] + extra
            rest = rest - extra
    return np.array(counts)


def bell_draw(stream_key, dims, deviation, reach, pieces=(), kind=jnp.bfloat16):
    factor_of = levels(stream_key, dims, pieces, -0.22, 0.18) if pieces else 1.0
    array = jax.random.normal(stream_key, dims, jnp.float32) * deviation * factor_of
    return jnp.minimum(jnp.maximum(array, -reach), reach).astype(kind)


def setup_inputs(seed: int = 0) -> dict:
    streams_of = jax.random.split(jax.random.key(seed), 6)
    out_grad = bell_draw(streams_of[0], (TOKENS, D), 1.0, 6.0, ((0, 256),))
    expert_ids_keys = jax.random.split(jax.random.fold_in(streams_of[1], 1), TOKENS // TOK_DEV)
    expert_ids_turns = jax.random.permutation(jax.random.fold_in(streams_of[1], 3), TOKENS // TOK_DEV)
    expert_ids = jax.vmap(lambda own, number: shared_out(jax.random.fold_in(streams_of[1], 2), own, number, TOK_DEV, EXPERTS, TOPK, CAP, 2))(expert_ids_keys, expert_ids_turns).reshape((TOKENS, TOPK))
    gate_weights = jnp.clip(jnp.exp(math.log(0.5) - 3.224016 * jax.random.uniform(streams_of[2], (TOKENS, TOPK), jnp.float32) ** levels(streams_of[2], (TOKENS, TOPK), ((0, 256),), -0.2, 0.2)), 0.019897461, 0.5).astype(jnp.bfloat16)
    saved_acts = bell_draw(streams_of[3], (N_DP, N_EXPERT, EXPERTS, CAP, 2 * FF_W), 1.5, 8.0, ((0, 16), (2, 16)))
    down_weight = bell_draw(streams_of[4], (EXPERTS, D, FF_W), D ** -0.5, 0.09375, ((0, 16), (1, 16)))
    return dict(out_grad=out_grad, expert_ids=expert_ids, gate_weights=gate_weights, saved_acts=saved_acts, down_weight=down_weight)


def slot_numbers(choice_rows):
    hits = jnp.sum((choice_rows[:, :, None] == jnp.arange(EXPERTS, dtype=jnp.int32)[None, None, :]).astype(jnp.int32), axis=1)
    before = (jnp.cumsum(hits, axis=0) - hits).astype(jnp.int32)
    return jnp.take_along_axis(before, choice_rows, axis=1).astype(jnp.int32)


def reference(out_grad, expert_ids, gate_weights, saved_acts, down_weight):
    sources = N_EXPERT
    grads = out_grad.reshape(N_DP, sources, TOK_DEV, D)
    choice_rows = expert_ids.reshape(N_DP, sources, TOK_DEV, TOPK)
    gates = gate_weights.reshape(N_DP, sources, TOK_DEV, TOPK)
    weight_f = down_weight.astype(jnp.float32)
    total_slots = sources * EXPERTS * CAP

    def one_group(carry, group):
        grad_row, id_row, gate_row, saved_row = group
        slots = jax.vmap(slot_numbers)(id_row)
        source_index = lax.broadcasted_iota(jnp.int32, id_row.shape, 0)
        target = ((source_index * EXPERTS + id_row) * CAP + slots).astype(jnp.int32)
        flat_target = target.reshape(-1)
        copies = jnp.broadcast_to(grad_row[:, :, None, :], id_row.shape + (D,)).reshape(-1, D)
        routed = jnp.zeros((total_slots, D), jnp.bfloat16).at[flat_target].set(copies).reshape(sources, EXPERTS, CAP, D)
        gate_slot = jnp.zeros((total_slots,), jnp.float32).at[flat_target].set(gate_row.reshape(-1).astype(jnp.float32)).reshape(sources, EXPERTS, CAP)
        gate_pre = saved_row[..., :FF_W].astype(jnp.float32)
        up_pre = saved_row[..., FF_W:].astype(jnp.float32)
        sigma = jax.nn.sigmoid(gate_pre)
        silu_val = gate_pre * sigma
        act = silu_val * up_pre
        back = jnp.einsum("secd,edf->secf", routed.astype(jnp.float32), weight_f)
        score = jnp.sum(back * act, axis=3)
        grad_act = gate_slot[..., None] * back
        d_gate = grad_act * up_pre * sigma * (1.0 + gate_pre * (1.0 - sigma))
        d_up = grad_act * silu_val
        pre_grad = jnp.concatenate([d_gate, d_up], axis=3).astype(jnp.bfloat16)
        act_low = act.astype(jnp.bfloat16)
        weighted = (gate_slot[..., None] * routed.astype(jnp.float32)).astype(jnp.bfloat16)
        share = jnp.einsum("secd,secf->edf", weighted.astype(jnp.float32), act_low.astype(jnp.float32))
        gate_row_grad = score.reshape(-1)[flat_target].reshape(id_row.shape)
        return carry + share, (pre_grad, gate_row_grad)

    start_sum = jnp.zeros((EXPERTS, D, FF_W), jnp.float32)
    summed, (pre_grads, gate_grad) = lax.scan(one_group, start_sum, (grads, choice_rows, gates, saved_acts))
    return pre_grads, summed.astype(jnp.bfloat16), gate_grad.reshape(TOKENS, TOPK)
```

```python
import jax
import jax.numpy as jnp
from jax import lax
from jax.experimental import pallas as pl
from jax.experimental.pallas import tpu as pltpu
from jax.sharding import PartitionSpec as P

MESH = pl.DeviceIdType.MESH
F32 = jnp.float32
BF16 = jnp.bfloat16

EXPERTS = 16
CAP = 48
TOK = 128
FF = 768
DZ = 256
NQ = 8
NZ = 8
NY = 4
DELTA = (4, 3, -3, 2, -2, 1, -1, 0)


def kernel(
    og_ref, ids_ref, saved_ref, w_ref,
    pre_ref, down_ref, gate_ref,
    tok, routed, stage, sel, gate, meta, wall, act_low, fac_g, fac_u, acc,
    rs_half, rs_out, rs_half_in, rs_in, fin_out, fin_in, own_sum, sc_out, sc_in,
    a_send, a_recv, s_send, s_recv, m_send, m_recv,
    bz_send, bz_recv, bx_send, bx_recv, c_send, c_recv, f_send, f_recv, g_send, g_recv,
):
    dp = lax.axis_index("dp")
    ex = lax.axis_index("expert")
    xl, z = dp // NZ, lax.rem(dp, NZ)
    y, xh, core = ex // 4, lax.rem(ex // 2, 2), lax.rem(ex, 2)

    def around_z(d):
        return lax.rem(z + (d + NZ), NZ)

    def around_y(d):
        return lax.rem(y + (d + NY), NY)

    def at_z(d):
        return {"dp": xl * NZ + around_z(d)}

    def at_y(d):
        return {"expert": (around_y(d) * 2 + xh) * 2 + core}

    x_mate = {"dp": (1 - xl) * NZ + z}
    h_mate = {"expert": (y * 2 + (1 - xh)) * 2 + core}
    c_mate = {"expert": (y * 2 + xh) * 2 + (1 - core)}

    def remote(src, dst, send, recv, to):
        return pltpu.make_async_remote_copy(
            src_ref=src, dst_ref=dst, send_sem=send, recv_sem=recv, device_id=to, device_id_type=MESH
        )

    barrier = pltpu.get_barrier_semaphore()

    def greet(i, carry):
        pl.semaphore_signal(
            barrier, inc=1, device_id={"expert": lax.rem(ex + i, EXPERTS)}, device_id_type=MESH
        )
        return carry

    lax.fori_loop(1, EXPERTS, greet, 0)
    for to in (x_mate, at_z(1), at_z(-1)):
        pl.semaphore_signal(barrier, inc=1, device_id=to, device_id_type=MESH)
    pl.semaphore_wait(barrier, EXPERTS + 2)

    me8 = y * 2 + xh
    ym8, yp8 = around_y(-1) * 2 + xh, around_y(1) * 2 + xh
    y2 = around_y(2) * 2 + xh
    flip = 1 - 2 * xh
    lower, upper = pl.ds(0, TOK // 2), pl.ds(TOK // 2, TOK // 2)

    def a_copy(kind, q, src8, rows, to):
        ref = tok.at[src8, q] if rows is None else tok.at[src8, q, rows]
        return remote(ref, ref, a_send.at[kind, q], a_recv.at[kind, q], to)

    def a_out(kind, q):
        return (
            lambda: a_copy(0, q, me8, None, h_mate),
            lambda: a_copy(1, q, me8, None, at_y(1)),
            lambda: a_copy(2, q, me8, None, at_y(-1)),
            lambda: a_copy(3, q, me8 + flip, None, at_y(1)),
            lambda: a_copy(4, q, me8 + flip, None, at_y(-1)),
            lambda: a_copy(5, q, ym8, lower, at_y(1)),
            lambda: a_copy(6, q, yp8, upper, at_y(-1)),
            lambda: a_copy(7, q, ym8 + flip, lower, at_y(1)),
            lambda: a_copy(8, q, yp8 + flip, upper, at_y(-1)),
        )[kind]()

    def a_in(kind, q):
        return (
            lambda: a_copy(0, q, me8 + flip, None, h_mate),
            lambda: a_copy(1, q, ym8, None, at_y(1)),
            lambda: a_copy(2, q, yp8, None, at_y(-1)),
            lambda: a_copy(3, q, ym8 + flip, None, at_y(1)),
            lambda: a_copy(4, q, yp8 + flip, None, at_y(-1)),
            lambda: a_copy(5, q, y2, lower, at_y(1)),
            lambda: a_copy(6, q, y2, upper, at_y(-1)),
            lambda: a_copy(7, q, y2 + flip, lower, at_y(1)),
            lambda: a_copy(8, q, y2 + flip, upper, at_y(-1)),
        )[kind]()

    def a_own(q):
        zq = around_z(DELTA[q])
        for col in range(2):
            tok[me8, q, :, col * DZ : (col + 1) * DZ] = og_ref[
                :, pl.ds(pl.multiple_of(col * NZ * DZ + zq * DZ, DZ), DZ)
            ]
        for kind in (0, 1, 2):
            a_out(kind, q).start()

    half = DZ // 2

    def bz_copy(way, step, to_send):
        sign = 1 if way == 0 else -1
        dist = step - 1 if to_send else step
        ref = wall.at[around_z(-sign * dist), xl]
        if step == 4:
            ref = ref.at[pl.ds(way * half, half)]
        return remote(ref, ref, bz_send.at[way, step - 1], bz_recv.at[way, step - 1], at_z(sign))

    def bx_copy(i, mine):
        ref = wall.at[around_z(i), xl if mine else 1 - xl]
        return remote(ref, ref, bx_send.at[i], bx_recv.at[i], x_mate)

    a_own(0)
    expert_row = lax.broadcasted_iota(jnp.int32, (EXPERTS, TOK), 0).astype(F32)
    hits = jnp.zeros((EXPERTS, TOK), F32)
    gates = jnp.zeros((EXPERTS, TOK), F32)
    for k in range(4):
        eq = expert_row == ids_ref[k : k + 1, :]
        hits = hits + jnp.where(eq, 1.0, 0.0)
        gates = gates + jnp.where(eq, ids_ref[4 + k : 5 + k, :], 0.0)
    earlier = (
        lax.broadcasted_iota(jnp.int32, (TOK, TOK), 0) < lax.broadcasted_iota(jnp.int32, (TOK, TOK), 1)
    )
    before = jnp.dot(
        hits.astype(BF16), jnp.where(earlier, 1.0, 0.0).astype(BF16), preferred_element_type=F32
    )
    meta[ex, 0:EXPERTS, :] = jnp.where(hits > 0.5, before, -1.0)
    meta[ex, EXPERTS : 2 * EXPERTS, :] = gates

    def m_copy(i, slot, to):
        return remote(meta.at[slot], meta.at[slot], m_send.at[i], m_recv.at[i], {"expert": to})

    def meta_send(i, carry):
        m_copy(i, ex, lax.rem(ex + i, EXPERTS)).start()
        return carry

    lax.fori_loop(1, EXPERTS, meta_send, 0)
    a_own(1)
    wall[z, xl] = w_ref[...]
    bz_copy(0, 1, True).start()
    bz_copy(1, 1, True).start()

    def factors(s, carry):
        row = lax.rem(s, 2) * 8 + s // 2
        for part in range(2):
            lanes = pl.ds(part * (FF // 2), FF // 2)
            g = saved_ref[s, :, part * (FF // 2) : (part + 1) * (FF // 2)].astype(F32)
            u = saved_ref[s, :, FF + part * (FF // 2) : FF + (part + 1) * (FF // 2)].astype(F32)
            sig = jax.nn.sigmoid(g)
            silu = g * sig
            act_low[row, :, lanes] = (silu * u).astype(BF16)
            fac_g[row, :, lanes] = u * sig * (1.0 + g * (1.0 - sig))
            fac_u[row, :, lanes] = silu
        return carry

    lax.fori_loop(0, 16, factors, 0)

    def meta_wait(i, carry):
        m_copy(i, lax.rem(ex - i + EXPERTS, EXPERTS), ex).wait_recv()
        return carry

    lax.fori_loop(1, EXPERTS, meta_wait, 0)
    cap_row = lax.broadcasted_iota(jnp.int32, (CAP, TOK), 0).astype(F32)

    def choose(s, carry):
        hit = cap_row == meta[s, pl.ds(ex, 1), :]
        value = jnp.where(hit, meta[s, pl.ds(EXPERTS + ex, 1), :], 0.0)
        row = lax.rem(s, 2) * 8 + s // 2
        gate[row] = jnp.broadcast_to(jnp.sum(value, axis=1, keepdims=True), (CAP, TOK))
        return carry

    lax.fori_loop(0, 16, choose, 0)

    def choose_both(s8, carry):
        s = s8 * 2 + core
        mate_ex = (y * 2 + xh) * 2 + (1 - core)
        mine = cap_row == meta[s, pl.ds(ex, 1), :]
        its = cap_row == meta[s, pl.ds(mate_ex, 1), :]
        sel[s8, 0:CAP, :] = jnp.where(mine, 1.0, 0.0).astype(BF16)
        sel[s8, CAP : 2 * CAP, :] = jnp.where(its, 1.0, 0.0).astype(BF16)
        return carry

    lax.fori_loop(0, 8, choose_both, 0)

    def s_copy(q, mine):
        c = core if mine else 1 - core
        return remote(stage.at[q], routed.at[q, c], s_send.at[q], s_recv.at[q], c_mate)

    def select(q):
        def one(s8, carry):
            got = jnp.dot(sel[s8], tok[s8, q], preferred_element_type=F32).astype(BF16)
            routed[q, core, s8] = got[0:CAP]
            stage[q, s8] = got[CAP : 2 * CAP]
            return carry

        lax.fori_loop(0, 8, one, 0)
        s_copy(q, True).start()

    def partial_sum(q, col):
        rows = routed[q, :, :, :, col * DZ : (col + 1) * DZ].reshape(16 * CAP, DZ).astype(F32)
        scale = gate[...].reshape(16 * CAP, TOK)[:, 0:1]
        weighted = (rows * scale).astype(BF16)
        return lax.dot_general(
            weighted,
            act_low[...].reshape(16 * CAP, FF),
            (((0,), (0,)), ((), ())),
            preferred_element_type=F32,
        )

    def c_half(way):
        return remote(
            rs_half.at[way], rs_half_in.at[way], c_send.at[way, 0], c_recv.at[way, 0], at_z(1 - 2 * way)
        )

    def c_full(way, hop):
        return remote(
            rs_out.at[way, hop - 1],
            rs_in.at[way, hop - 1],
            c_send.at[way, hop],
            c_recv.at[way, hop],
            at_z(1 - 2 * way),
        )

    def reduce(q):
        if q == 0:
            for col in range(2):
                part = partial_sum(q, col)
                for way in range(2):
                    rs_half[way, col] = part[way * half : (way + 1) * half].astype(BF16)
            c_half(0).start()
            c_half(1).start()
            return
        if q == 7:
            return
        way, hop = (q + 1) % 2, (q + 1) // 2
        if hop == 1:
            c_half(way).wait_recv()
        else:
            c_full(way, hop - 1).wait_recv()
        for col in range(2):
            part = partial_sum(q, col)
            if hop == 1:
                mid = slice(way * half, (way + 1) * half)
                rest = slice((1 - way) * half, (2 - way) * half)
                rs_out[way, 0, col, mid] = (part[mid] + rs_half_in[way, col].astype(F32)).astype(BF16)
                rs_out[way, 0, col, rest] = part[rest].astype(BF16)
            else:
                rs_out[way, hop - 1, col] = (part + rs_in[way, hop - 2, col].astype(F32)).astype(BF16)
        c_full(way, hop).start()

    def f_copy():
        return remote(fin_out, fin_in, f_send, f_recv, x_mate)

    for t in range(NQ + 3):
        if 0 < t and t + 1 < NQ:
            a_own(t + 1)
        if t < NQ:
            a_in(0, t).wait_recv()
            a_out(3, t).start()
            a_out(4, t).start()
            a_in(1, t).wait_recv()
            a_out(5, t).start()
            a_in(2, t).wait_recv()
            a_out(6, t).start()
        if 1 <= t <= 3:
            for way in range(2):
                bz_copy(way, t, False).wait_recv()
                bz_copy(way, t + 1, True).start()
        if t == 4:
            for way in range(2):
                bz_copy(way, 4, False).wait_recv()
        bx = {1: (0,), 2: (1,), 3: (7,), 4: (2, 6), 5: (3,), 6: (5,), 7: (4,)}.get(t, ())
        for i in bx:
            bx_copy(i, True).start()
        if 0 <= t - 1 < NQ:
            a_in(3, t - 1).wait_recv()
            a_out(7, t - 1).start()
            a_in(4, t - 1).wait_recv()
            a_out(8, t - 1).start()
        if 0 <= t - 2 < NQ:
            for kind in (5, 6, 7, 8):
                a_in(kind, t - 2).wait_recv()
            select(t - 2)
        if 0 <= t - 3 < NQ:
            s_copy(t - 3, False).wait_recv()
            reduce(t - 3)

    for i in range(NZ):
        bx_copy(i, False).wait_recv()

    def back(c):
        acc[...] = jnp.zeros_like(acc)
        for q in range(NQ):
            zq = around_z(DELTA[q])
            acc[...] += jnp.dot(
                routed[q, c].reshape(8 * CAP, 2 * DZ),
                wall[zq].reshape(2 * DZ, FF),
                preferred_element_type=F32,
            )

    def g_copy(i, src, dst, to):
        return remote(sc_out.at[src], sc_in.at[dst], g_send.at[i], g_recv.at[i], {"expert": to})

    def finish(c):
        def one(s8, carry):
            s = s8 * 2 + c
            row = c * 8 + s8
            out = acc[pl.ds(pl.multiple_of(s8 * CAP, CAP), CAP), :]
            scale = gate[row][:, 0:1]
            grad = out * scale
            silu = fac_u[row]
            u = saved_ref[s, :, FF : 2 * FF].astype(F32)
            pre_ref[s, :, 0:FF] = (grad * fac_g[row]).astype(BF16)
            pre_ref[s, :, FF : 2 * FF] = (grad * silu).astype(BF16)
            score = jnp.sum(out * (silu * u), axis=1, keepdims=True)
            sc_out[s] = jnp.broadcast_to(score, (CAP, TOK))
            return carry

        lax.fori_loop(0, 8, one, 0)

    back(0)

    c_full(0, 3).wait_recv()
    c_full(1, 3).wait_recv()

    def last(col):
        return partial_sum(7, col) + rs_in[0, 2, col].astype(F32) + rs_in[1, 2, col].astype(F32)

    for col in range(2):
        own_sum[col] = last(col)
    fin_out[...] = own_sum[1 - xl].astype(BF16)
    f_copy().start()

    finish(0)
    back(1)
    finish(1)

    def score_send(i, carry):
        to = lax.rem(ex + i, EXPERTS)
        g_copy(i, to, ex, to).start()
        return carry

    lax.fori_loop(1, EXPERTS, score_send, 0)
    sc_in[ex] = sc_out[ex]

    f_copy().wait_recv()
    down_ref[...] = (own_sum[xl] + fin_in[...].astype(F32)).astype(BF16)

    def score_wait(i, carry):
        g_copy(i, ex, lax.rem(ex - i + EXPERTS, EXPERTS), ex).wait_recv()
        return carry

    lax.fori_loop(1, EXPERTS, score_wait, 0)

    rows = [jnp.zeros((1, TOK), F32) for _ in range(4)]
    for e in range(EXPERTS):
        hit = cap_row == meta[ex, e : e + 1, :]
        value = jnp.sum(jnp.where(hit, sc_in[e], 0.0), axis=0, keepdims=True)
        for k in range(4):
            rows[k] = rows[k] + jnp.where(ids_ref[k : k + 1, :] == float(e), value, 0.0)
    for k in range(4):
        gate_ref[k : k + 1, :] = rows[k]
        gate_ref[4 + k : 5 + k, :] = rows[k]

    def drain_peers(i, carry):
        to = lax.rem(ex + i, EXPERTS)
        m_copy(i, ex, to).wait_send()
        g_copy(i, to, ex, to).wait_send()
        return carry

    lax.fori_loop(1, EXPERTS, drain_peers, 0)
    for q in range(NQ):
        for kind in range(9):
            a_out(kind, q).wait_send()
        s_copy(q, True).wait_send()
        bx_copy(q, True).wait_send()
    for way in range(2):
        for step in range(1, 5):
            bz_copy(way, step, True).wait_send()
        c_half(way).wait_send()
        for hop in range(1, 4):
            c_full(way, hop).wait_send()
    f_copy().wait_send()


def shards(out_grad, expert_ids, gate_weights, saved_acts, down_weight):
    small = jnp.concatenate([expert_ids.astype(F32), gate_weights.astype(F32)], axis=1).T
    vmem = pl.BlockSpec(memory_space=pltpu.VMEM)
    dma = pltpu.SemaphoreType.DMA
    pre, down, gate_t = pl.pallas_call(
        kernel,
        out_shape=(
            jax.ShapeDtypeStruct((EXPERTS, CAP, 2 * FF), BF16),
            jax.ShapeDtypeStruct((DZ, FF), BF16),
            jax.ShapeDtypeStruct((8, TOK), F32),
        ),
        in_specs=[vmem] * 4,
        out_specs=(vmem,) * 3,
        scratch_shapes=[
            pltpu.VMEM((8, NQ, TOK, 2 * DZ), BF16),
            pltpu.VMEM((NQ, 2, 8, CAP, 2 * DZ), BF16),
            pltpu.VMEM((NQ, 8, CAP, 2 * DZ), BF16),
            pltpu.VMEM((8, 2 * CAP, TOK), BF16),
            pltpu.VMEM((16, CAP, TOK), F32),
            pltpu.VMEM((16, 2 * EXPERTS, TOK), F32),
            pltpu.VMEM((NZ, 2, DZ, FF), BF16),
            pltpu.VMEM((16, CAP, FF), BF16),
            pltpu.VMEM((16, CAP, FF), F32),
            pltpu.VMEM((16, CAP, FF), F32),
            pltpu.VMEM((8 * CAP, FF), F32),
            pltpu.VMEM((2, 2, DZ // 2, FF), BF16),
            pltpu.VMEM((2, 3, 2, DZ, FF), BF16),
            pltpu.VMEM((2, 2, DZ // 2, FF), BF16),
            pltpu.VMEM((2, 3, 2, DZ, FF), BF16),
            pltpu.VMEM((DZ, FF), BF16),
            pltpu.VMEM((DZ, FF), BF16),
            pltpu.VMEM((2, DZ, FF), F32),
            pltpu.VMEM((16, CAP, TOK), F32),
            pltpu.VMEM((16, CAP, TOK), F32),
            dma((9, NQ)), dma((9, NQ)),
            dma((NQ,)), dma((NQ,)),
            dma((EXPERTS,)), dma((EXPERTS,)),
            dma((2, 4)), dma((2, 4)),
            dma((NZ,)), dma((NZ,)),
            dma((2, 4)), dma((2, 4)),
            dma(()), dma(()),
            dma((EXPERTS,)), dma((EXPERTS,)),
        ],
        compiler_params=pltpu.CompilerParams(
            collective_id=0, has_side_effects=True, vmem_limit_bytes=60 * 1024 * 1024
        ),
    )(out_grad, small, saved_acts[0, :, 0], down_weight[0])
    return pre[None, :, None], down[None], gate_t[:4].T


def solution(mesh):
    placed = (
        P(("dp", "expert"), None),
        P(("dp", "expert"), None),
        P(("dp", "expert"), None),
        P("dp", None, "expert", None, None),
        P("expert", "dp", None),
    )
    return jax.shard_map(
        shards,
        mesh=mesh,
        in_specs=placed,
        out_specs=(
            P("dp", None, "expert", None, None),
            P("expert", "dp", None),
            P(("dp", "expert"), None),
        ),
        check_vma=False,
    )
```

```python
import jax
import jax.numpy as jnp
from jax import lax
from jax.experimental import pallas as pl
from jax.experimental.pallas import tpu as pltpu
from jax.sharding import PartitionSpec as P

MESH = pl.DeviceIdType.MESH
F32 = jnp.float32
BF16 = jnp.bfloat16

EXPERTS = 16
CAP = 48
TOK = 128
FF = 768
DZ = 256
NQ = 8
NZ = 8
NY = 4
PIECES = (
    ((4, 0), (4, 1)),
    ((3, 0), (-3, 0)),
    ((3, 1), (-3, 1)),
    ((2, 0), (-2, 0)),
    ((2, 1), (-2, 1)),
    ((1, 0), (-1, 0)),
    ((1, 1), (-1, 1)),
    ((0, 0), (0, 1)),
)


def kernel(
    og_ref, ids_ref, saved_hbm, w_ref,
    pre_hbm, down_ref, gate_ref,
    saved_ref, pre_ref, tok, routed, stage, sel, gate, meta_low, meta, wall, act_low, fac_g, fac_u, acc,
    rs_half, rs_out, rs_half_in, rs_in, fin_out, fin_in, part, sc_out, sc_in,
    a_send, a_recv, s_send, s_recv, m_send, m_recv,
    bz_send, bz_recv, bx_send, bx_recv, bn_send, bn_recv, c_send, c_recv, f_send, f_recv,
    g_send, g_recv, og_sem, w_sem, saved_sem, pre_sem,
):
    dp = lax.axis_index("dp")
    ex = lax.axis_index("expert")
    xl, z = dp // NZ, lax.rem(dp, NZ)
    y, xh, core = ex // 4, lax.rem(ex // 2, 2), lax.rem(ex, 2)

    def around_z(d):
        return lax.rem(z + (d + NZ), NZ)

    def around_y(d):
        return lax.rem(y + (d + NY), NY)

    def at_z(d):
        return {"dp": xl * NZ + around_z(d)}

    def at_y(d):
        return {"expert": (around_y(d) * 2 + xh) * 2 + core}

    x_mate = {"dp": (1 - xl) * NZ + z}
    h_mate = {"expert": (y * 2 + (1 - xh)) * 2 + core}
    c_mate = {"expert": (y * 2 + xh) * 2 + (1 - core)}

    def remote(src, dst, send, recv, to):
        return pltpu.make_async_remote_copy(
            src_ref=src, dst_ref=dst, send_sem=send, recv_sem=recv, device_id=to, device_id_type=MESH
        )

    barrier = pltpu.get_barrier_semaphore()

    def greet(i, carry):
        pl.semaphore_signal(
            barrier, inc=1, device_id={"expert": lax.rem(ex + i, EXPERTS)}, device_id_type=MESH
        )
        return carry

    lax.fori_loop(1, EXPERTS, greet, 0)
    for to in (x_mate, at_z(1), at_z(-1)):
        pl.semaphore_signal(barrier, inc=1, device_id=to, device_id_type=MESH)

    me8 = y * 2 + xh

    def column(order):
        return 1 - xl if order == 0 else xl

    def og_copy(q, j):
        dist, order = PIECES[q][j]
        cols = pl.ds(pl.multiple_of((column(order) * NZ + around_z(dist)) * DZ, DZ), DZ)
        return pltpu.make_async_copy(
            og_ref.at[:, cols], tok.at[me8, q, :, pl.ds(j * DZ, DZ)], og_sem.at[q, j]
        )

    w_copy = pltpu.make_async_copy(w_ref, wall.at[z, xl], w_sem)
    saved_copy = pltpu.make_async_copy(saved_hbm, saved_ref, saved_sem)
    for q in range(NQ):
        for col in range(2):
            og_copy(q, col).start()
        if q == 1:
            w_copy.start()
    saved_copy.start()
    expert_row = lax.broadcasted_iota(jnp.int32, (EXPERTS, TOK), 0).astype(F32)
    hits = jnp.zeros((EXPERTS, TOK), F32)
    gates = jnp.zeros((EXPERTS, TOK), F32)
    for k in range(4):
        eq = expert_row == ids_ref[k : k + 1, :]
        hits = hits + jnp.where(eq, 1.0, 0.0)
        gates = gates + jnp.where(eq, ids_ref[4 + k : 5 + k, :], 0.0)
    earlier = (
        lax.broadcasted_iota(jnp.int32, (TOK, TOK), 0) < lax.broadcasted_iota(jnp.int32, (TOK, TOK), 1)
    )
    before = jnp.dot(
        hits.astype(BF16), jnp.where(earlier, 1.0, 0.0).astype(BF16), preferred_element_type=F32
    )
    meta_low[ex, 0:EXPERTS, :] = jnp.where(hits > 0.5, before, -1.0).astype(BF16)
    meta_low[ex, EXPERTS : 2 * EXPERTS, :] = gates.astype(BF16)

    pl.semaphore_wait(barrier, EXPERTS + 2)

    def m_copy(i, slot, to):
        return remote(meta_low.at[slot], meta_low.at[slot], m_send.at[i], m_recv.at[i], {"expert": to})

    def meta_send(i, carry):
        m_copy(i, ex, lax.rem(ex + i, EXPERTS)).start()
        return carry

    lax.fori_loop(1, EXPERTS, meta_send, 0)

    ym8, yp8 = around_y(-1) * 2 + xh, around_y(1) * 2 + xh
    y2 = around_y(2) * 2 + xh
    flip = 1 - 2 * xh
    lower, upper = pl.ds(0, TOK // 2), pl.ds(TOK // 2, TOK // 2)

    def a_copy(kind, q, src8, rows, to):
        ref = tok.at[src8, q] if rows is None else tok.at[src8, q, rows]
        return remote(ref, ref, a_send.at[kind, q], a_recv.at[kind, q], to)

    def a_out(kind, q):
        return (
            lambda: a_copy(0, q, me8, None, h_mate),
            lambda: a_copy(1, q, me8, None, at_y(1)),
            lambda: a_copy(2, q, me8, None, at_y(-1)),
            lambda: a_copy(3, q, me8 + flip, None, at_y(1)),
            lambda: a_copy(4, q, me8 + flip, None, at_y(-1)),
            lambda: a_copy(5, q, ym8, lower, at_y(1)),
            lambda: a_copy(6, q, yp8, upper, at_y(-1)),
            lambda: a_copy(7, q, ym8 + flip, lower, at_y(1)),
            lambda: a_copy(8, q, yp8 + flip, upper, at_y(-1)),
        )[kind]()

    def a_in(kind, q):
        return (
            lambda: a_copy(0, q, me8 + flip, None, h_mate),
            lambda: a_copy(1, q, ym8, None, at_y(1)),
            lambda: a_copy(2, q, yp8, None, at_y(-1)),
            lambda: a_copy(3, q, ym8 + flip, None, at_y(1)),
            lambda: a_copy(4, q, yp8 + flip, None, at_y(-1)),
            lambda: a_copy(5, q, y2, lower, at_y(1)),
            lambda: a_copy(6, q, y2, upper, at_y(-1)),
            lambda: a_copy(7, q, y2 + flip, lower, at_y(1)),
            lambda: a_copy(8, q, y2 + flip, upper, at_y(-1)),
        )[kind]()

    def a_own(q):
        for kind in (1, 2):
            a_out(kind, q).start()

    half = DZ // 2

    def bz_copy(way, step, to_send):
        sign = 1 if way == 0 else -1
        dist = step - 1 if to_send else step
        ref = wall.at[around_z(-sign * dist), xl]
        if step == 4:
            ref = ref.at[pl.ds(way * half, half)]
        return remote(ref, ref, bz_send.at[way, step - 1], bz_recv.at[way, step - 1], at_z(sign))

    def bx_copy(i, mine):
        ref = wall.at[around_z(i), xl if mine else 1 - xl]
        if i in (1, 7):
            ref = ref.at[pl.ds(half, half)]
        return remote(ref, ref, bx_send.at[i], bx_recv.at[i], x_mate)

    def bn_copy(way, to_send):
        sign = 1 if way == 0 else -1
        ref = wall.at[around_z(0 if to_send else -sign), 1 - xl, pl.ds(0, half)]
        return remote(ref, ref, bn_send.at[way], bn_recv.at[way], at_z(sign))

    for q in range(NQ):
        for j in range(2):
            og_copy(q, j).wait()
        a_out(0, q).start()
        if q < 2:
            a_own(q)
        if q == 0:
            w_copy.wait()
            bz_copy(0, 1, True).start()
            bz_copy(1, 1, True).start()
        if q == 2:
            bx_copy(0, True).start()

    def factors(s, carry):
        row = lax.rem(s, 2) * 8 + s // 2
        for part in range(2):
            lanes = pl.ds(part * (FF // 2), FF // 2)
            g = saved_ref[s, :, part * (FF // 2) : (part + 1) * (FF // 2)].astype(F32)
            u = saved_ref[s, :, FF + part * (FF // 2) : FF + (part + 1) * (FF // 2)].astype(F32)
            sig = jax.nn.sigmoid(g)
            silu = g * sig
            act_low[row, :, lanes] = (silu * u).astype(BF16)
            fac_g[row, :, lanes] = u * sig * (1.0 + g * (1.0 - sig))
            fac_u[row, :, lanes] = silu
        return carry

    saved_copy.wait()
    lax.fori_loop(0, 4, factors, 0)

    def meta_wait(i, carry):
        m_copy(i, lax.rem(ex - i + EXPERTS, EXPERTS), ex).wait_recv()
        return carry

    cap_row = lax.broadcasted_iota(jnp.int32, (CAP, TOK), 0).astype(F32)

    def choose(s, carry):
        hit = cap_row == meta[s, pl.ds(ex, 1), :]
        value = jnp.where(hit, meta[s, pl.ds(EXPERTS + ex, 1), :], 0.0)
        row = lax.rem(s, 2) * 8 + s // 2
        gate[row] = jnp.broadcast_to(jnp.sum(value, axis=1, keepdims=True), (CAP, TOK))
        return carry


    def choose_both(s8, carry):
        s = s8 * 2 + core
        mate_ex = (y * 2 + xh) * 2 + (1 - core)
        mine = cap_row == meta[s, pl.ds(ex, 1), :]
        its = cap_row == meta[s, pl.ds(mate_ex, 1), :]
        sel[s8, 0:CAP, :] = jnp.where(mine, 1.0, 0.0).astype(BF16)
        sel[s8, CAP : 2 * CAP, :] = jnp.where(its, 1.0, 0.0).astype(BF16)
        return carry

    def choose_rows():
        lax.fori_loop(1, EXPERTS, meta_wait, 0)
        meta[...] = meta_low[...].astype(F32)
        lax.fori_loop(0, 16, choose, 0)
        lax.fori_loop(0, 8, choose_both, 0)

    def s_copy(q, mine):
        c = core if mine else 1 - core
        return remote(stage.at[q], routed.at[q, c], s_send.at[q], s_recv.at[q], c_mate)

    def select(q):
        def one(s8, carry):
            got = jnp.dot(sel[s8], tok[s8, q], preferred_element_type=F32).astype(BF16)
            routed[q, core, s8] = got[0:CAP]
            stage[q, s8] = got[CAP : 2 * CAP]
            return carry

        lax.fori_loop(0, 8, one, 0)
        s_copy(q, True).start()

    def partial_sum(q, j):
        rows = routed[q, :, :, :, j * DZ : (j + 1) * DZ].reshape(16 * CAP, DZ).astype(F32)
        scale = gate[...].reshape(16 * CAP, TOK)[:, 0:1]
        weighted = (rows * scale).astype(BF16)
        part[j] = lax.dot_general(
            weighted,
            act_low[...].reshape(16 * CAP, FF),
            (((0,), (0,)), ((), ())),
            preferred_element_type=F32,
        )

    def c_half(way, order):
        return remote(
            rs_half.at[way, order],
            rs_half_in.at[way, order],
            c_send.at[way, 0, order],
            c_recv.at[way, 0, order],
            at_z(1 - 2 * way),
        )

    def c_full(way, hop, order):
        return remote(
            rs_out.at[way, hop - 1, order],
            rs_in.at[way, hop - 1, order],
            c_send.at[way, hop, order],
            c_recv.at[way, hop, order],
            at_z(1 - 2 * way),
        )

    def reduce(q):
        for j in range(2):
            partial_sum(q, j)
            if q == 0:
                for way in range(2):
                    rs_half[way, j] = part[j, way * half : (way + 1) * half, :].astype(BF16)
                    c_half(way, j).start()

    def chain(q):
        order, hop = (q - 1) % 2, (q + 1) // 2
        for way in range(2):
            if hop == 1:
                c_half(way, order).wait_recv()
                mid = slice(way * half, (way + 1) * half)
                rest = slice((1 - way) * half, (2 - way) * half)
                rs_out[way, 0, order, mid] = (
                    part[way, mid, :] + rs_half_in[way, order].astype(F32)
                ).astype(BF16)
                rs_out[way, 0, order, rest] = part[way, rest, :].astype(BF16)
            else:
                c_full(way, hop - 1, order).wait_recv()
                rs_out[way, hop - 1, order] = (
                    part[way] + rs_in[way, hop - 2, order].astype(F32)
                ).astype(BF16)
            c_full(way, hop, order).start()

    def f_copy():
        return remote(fin_out, fin_in, f_send, f_recv, x_mate)

    def back(q):
        for c in range(2):
            rows = slice(c * 8 * CAP, (c + 1) * 8 * CAP)
            got = acc[rows, :]
            for j in range(2):
                dist, order = PIECES[q][j]
                got = got + jnp.dot(
                    routed[q, c, :, :, j * DZ : (j + 1) * DZ].reshape(8 * CAP, DZ),
                    wall[around_z(dist), column(order)],
                    preferred_element_type=F32,
                )
            acc[rows, :] = got

    acc[...] = jnp.zeros_like(acc)

    for t in range(NQ + 2):
        if t < NQ:
            a_in(0, t).wait_recv()
            a_out(3, t).start()
            a_out(4, t).start()
            a_in(1, t).wait_recv()
            a_out(5, t).start()
            a_in(2, t).wait_recv()
            a_out(6, t).start()
        for q in {0: (2,), 1: (3, 4)}.get(t, (t + 3,)):
            if q < NQ:
                a_own(q)
        if 0 <= t - 1 < NQ:
            a_in(3, t - 1).wait_recv()
            a_out(7, t - 1).start()
            a_in(4, t - 1).wait_recv()
            a_out(8, t - 1).start()
        if t in (1, 2, 3):
            for way in range(2):
                bz_copy(way, t, False).wait_recv()
                bz_copy(way, t + 1, True).start()
        if t == 2:
            bx_copy(0, False).wait_recv()
            bn_copy(0, True).start()
            bn_copy(1, True).start()
        if t == 5:
            bz_copy(0, 4, False).wait_recv()
            bz_copy(1, 4, False).wait_recv()
        for i in {1: (1, 7), 2: (2, 6), 3: (3, 5), 5: (4,)}.get(t, ()):
            bx_copy(i, True).start()
        if t < 2:
            lax.fori_loop(4 + 6 * t, 10 + 6 * t, factors, 0)
        if t == 1:
            choose_rows()
        if t == 7:
            for i in (1, 7, 2, 6):
                bx_copy(i, False).wait_recv()
            bn_copy(0, False).wait_recv()
            bn_copy(1, False).wait_recv()
        if 0 <= t - 2 < NQ:
            for kind in (5, 6, 7, 8):
                a_in(kind, t - 2).wait_recv()
            select(t - 2)
            if t - 3 >= 1:
                chain(t - 3)
            if t == 7:
                back(3)
            if t == 8:
                back(4)
                back(5)
            s_copy(t - 2, False).wait_recv()
            reduce(t - 2)

    def g_copy(i, src, dst, to):
        return remote(sc_out.at[src], sc_in.at[dst], g_send.at[i], g_recv.at[i], {"expert": to})

    def finish(c):
        def one(s8, carry):
            s = s8 * 2 + c
            row = c * 8 + s8
            out = acc[pl.ds(pl.multiple_of(row * CAP, CAP), CAP), :]
            scale = gate[row][:, 0:1]
            grad = out * scale
            silu = fac_u[row]
            u = saved_ref[s, :, FF : 2 * FF].astype(F32)
            pre_ref[s, :, 0:FF] = (grad * fac_g[row]).astype(BF16)
            pre_ref[s, :, FF : 2 * FF] = (grad * silu).astype(BF16)
            score = jnp.sum(out * (silu * u), axis=1, keepdims=True)
            sc_out[s] = jnp.broadcast_to(score, (CAP, TOK))
            return carry

        lax.fori_loop(0, 8, one, 0)

    def last(order):
        c_full(0, 3, order).wait_recv()
        c_full(1, 3, order).wait_recv()
        return part[order] + rs_in[0, 2, order].astype(F32) + rs_in[1, 2, order].astype(F32)

    back(6)
    back(7)
    fin_out[...] = last(0).astype(BF16)
    f_copy().start()
    bx_copy(3, False).wait_recv()
    bx_copy(5, False).wait_recv()
    back(1)
    back(2)
    bx_copy(4, False).wait_recv()
    back(0)

    def pre_copy(c, s8):
        ref = s8 * 2 + c
        return pltpu.make_async_copy(pre_ref.at[ref], pre_hbm.at[ref], pre_sem.at[ref])

    def pre_out(c):
        for s8 in range(8):
            pre_copy(c, s8).start()

    finish(0)
    pre_out(0)
    finish(1)
    pre_out(1)

    def score_send(i, carry):
        to = lax.rem(ex + i, EXPERTS)
        g_copy(i, to, ex, to).start()
        return carry

    lax.fori_loop(1, EXPERTS, score_send, 0)
    sc_in[ex] = sc_out[ex]

    own = last(1)
    f_copy().wait_recv()
    down_ref[...] = (own + fin_in[...].astype(F32)).astype(BF16)

    def score_wait(i, carry):
        g_copy(i, ex, lax.rem(ex - i + EXPERTS, EXPERTS), ex).wait_recv()
        return carry

    lax.fori_loop(1, EXPERTS, score_wait, 0)

    rows = [jnp.zeros((1, TOK), F32) for _ in range(4)]
    for e in range(EXPERTS):
        hit = cap_row == meta[ex, e : e + 1, :]
        value = jnp.sum(jnp.where(hit, sc_in[e], 0.0), axis=0, keepdims=True)
        for k in range(4):
            rows[k] = rows[k] + jnp.where(ids_ref[k : k + 1, :] == float(e), value, 0.0)
    for k in range(4):
        gate_ref[k : k + 1, :] = rows[k]
        gate_ref[4 + k : 5 + k, :] = rows[k]

    def drain_peers(i, carry):
        to = lax.rem(ex + i, EXPERTS)
        m_copy(i, ex, to).wait_send()
        g_copy(i, to, ex, to).wait_send()
        return carry

    lax.fori_loop(1, EXPERTS, drain_peers, 0)
    for q in range(NQ):
        for kind in range(9):
            a_out(kind, q).wait_send()
        s_copy(q, True).wait_send()
        bx_copy(q, True).wait_send()
        for c in range(2):
            pre_copy(c, q).wait()
    for way in range(2):
        for step in range(1, 5):
            bz_copy(way, step, True).wait_send()
        bn_copy(way, True).wait_send()
        for order in range(2):
            c_half(way, order).wait_send()
            for hop in range(1, 4):
                c_full(way, hop, order).wait_send()
    f_copy().wait_send()


def shards(out_grad, expert_ids, gate_weights, saved_acts, down_weight):
    small = jnp.concatenate([expert_ids.astype(F32), gate_weights.astype(F32)], axis=1).T
    vmem = pl.BlockSpec(memory_space=pltpu.VMEM)
    hbm = pl.BlockSpec(memory_space=pl.ANY)
    dma = pltpu.SemaphoreType.DMA
    pre, down, gate_t = pl.pallas_call(
        kernel,
        out_shape=(
            jax.ShapeDtypeStruct((EXPERTS, CAP, 2 * FF), BF16),
            jax.ShapeDtypeStruct((DZ, FF), BF16),
            jax.ShapeDtypeStruct((8, TOK), F32),
        ),
        in_specs=[hbm, vmem, hbm, hbm],
        out_specs=(hbm, vmem, vmem),
        scratch_shapes=[
            pltpu.VMEM((EXPERTS, CAP, 2 * FF), BF16),
            pltpu.VMEM((EXPERTS, CAP, 2 * FF), BF16),
            pltpu.VMEM((8, NQ, TOK, 2 * DZ), BF16),
            pltpu.VMEM((NQ, 2, 8, CAP, 2 * DZ), BF16),
            pltpu.VMEM((NQ, 8, CAP, 2 * DZ), BF16),
            pltpu.VMEM((8, 2 * CAP, TOK), BF16),
            pltpu.VMEM((16, CAP, TOK), F32),
            pltpu.VMEM((16, 2 * EXPERTS, TOK), BF16),
            pltpu.VMEM((16, 2 * EXPERTS, TOK), F32),
            pltpu.VMEM((NZ, 2, DZ, FF), BF16),
            pltpu.VMEM((16, CAP, FF), BF16),
            pltpu.VMEM((16, CAP, FF), F32),
            pltpu.VMEM((16, CAP, FF), F32),
            pltpu.VMEM((16 * CAP, FF), F32),
            pltpu.VMEM((2, 2, DZ // 2, FF), BF16),
            pltpu.VMEM((2, 3, 2, DZ, FF), BF16),
            pltpu.VMEM((2, 2, DZ // 2, FF), BF16),
            pltpu.VMEM((2, 3, 2, DZ, FF), BF16),
            pltpu.VMEM((DZ, FF), BF16),
            pltpu.VMEM((DZ, FF), BF16),
            pltpu.VMEM((2, DZ, FF), F32),
            pltpu.VMEM((16, CAP, TOK), F32),
            pltpu.VMEM((16, CAP, TOK), F32),
            dma((9, NQ)), dma((9, NQ)),
            dma((NQ,)), dma((NQ,)),
            dma((EXPERTS,)), dma((EXPERTS,)),
            dma((2, 4)), dma((2, 4)),
            dma((NZ,)), dma((NZ,)),
            dma((2,)), dma((2,)),
            dma((2, 4, 2)), dma((2, 4, 2)),
            dma(()), dma(()),
            dma((EXPERTS,)), dma((EXPERTS,)),
            dma((NQ, 2)), dma(()), dma(()), dma((EXPERTS,)),
        ],
        compiler_params=pltpu.CompilerParams(
            collective_id=0, has_side_effects=True, vmem_limit_bytes=60 * 1024 * 1024
        ),
    )(out_grad, small, saved_acts[0, :, 0], down_weight[0])
    return pre[None, :, None], down[None], gate_t[:4].T


def solution(mesh):
    placed = (
        P(("dp", "expert"), None),
        P(("dp", "expert"), None),
        P(("dp", "expert"), None),
        P("dp", None, "expert", None, None),
        P("expert", "dp", None),
    )
    return jax.shard_map(
        shards,
        mesh=mesh,
        in_specs=placed,
        out_specs=(
            P("dp", None, "expert", None, None),
            P("expert", "dp", None),
            P(("dp", "expert"), None),
        ),
        check_vma=False,
    )
```

```python
import jax
import jax.numpy as jnp
from jax import lax
from jax.experimental import pallas as pl
from jax.experimental.pallas import tpu as pltpu
from jax.sharding import PartitionSpec as P

MESH = pl.DeviceIdType.MESH
F32 = jnp.float32
BF16 = jnp.bfloat16

EXPERTS = 16
CAP = 48
TOK = 128
FF = 768
DZ = 256
NQ = 8
NZ = 8
NY = 4
PIECES = (
    ((4, 0), (4, 1)),
    ((3, 0), (-3, 0)),
    ((3, 1), (-3, 1)),
    ((2, 0), (-2, 0)),
    ((2, 1), (-2, 1)),
    ((1, 0), (-1, 0)),
    ((1, 1), (-1, 1)),
    ((0, 0), (0, 1)),
)


def kernel(
    og_ref, ids_ref, weights_ref, saved_hbm, w_ref,
    pre_hbm, down_ref, gate_ref,
    saved_ref, pre_ref, tok, routed, stage, sel, gate, meta_low, meta, wall, act_low, fac_g, fac_u, acc,
    rs_half, rs_out, rs_half_in, rs_in, fin_out, fin_in, part, sc_out, sc_in,
    a_send, a_recv, s_send, s_recv, m_send, m_recv,
    bz_send, bz_recv, bx_send, bx_recv, bn_send, bn_recv, c_send, c_recv, f_send, f_recv,
    g_send, g_recv, og_sem, w_sem, saved_sem, pre_sem,
):
    dp = lax.axis_index("dp")
    ex = lax.axis_index("expert")
    xl, z = dp // NZ, lax.rem(dp, NZ)
    y, xh, core = ex // 4, lax.rem(ex // 2, 2), lax.rem(ex, 2)

    def around_z(d):
        return lax.rem(z + (d + NZ), NZ)

    def around_y(d):
        return lax.rem(y + (d + NY), NY)

    def at_z(d):
        return {"dp": xl * NZ + around_z(d)}

    def at_y(d):
        return {"expert": (around_y(d) * 2 + xh) * 2 + core}

    x_mate = {"dp": (1 - xl) * NZ + z}
    h_mate = {"expert": (y * 2 + (1 - xh)) * 2 + core}
    c_mate = {"expert": (y * 2 + xh) * 2 + (1 - core)}

    def remote(src, dst, send, recv, to):
        return pltpu.make_async_remote_copy(
            src_ref=src, dst_ref=dst, send_sem=send, recv_sem=recv, device_id=to, device_id_type=MESH
        )

    barrier = pltpu.get_barrier_semaphore()

    def greet(i, carry):
        pl.semaphore_signal(
            barrier, inc=1, device_id={"expert": lax.rem(ex + i, EXPERTS)}, device_id_type=MESH
        )
        return carry

    lax.fori_loop(1, EXPERTS, greet, 0)
    for to in (x_mate, at_z(1), at_z(-1)):
        pl.semaphore_signal(barrier, inc=1, device_id=to, device_id_type=MESH)

    me8 = y * 2 + xh

    def column(order):
        return 1 - xl if order == 0 else xl

    def og_copy(q, j):
        dist, order = PIECES[q][j]
        cols = pl.ds(pl.multiple_of((column(order) * NZ + around_z(dist)) * DZ, DZ), DZ)
        return pltpu.make_async_copy(
            og_ref.at[:, cols], tok.at[me8, q, :, pl.ds(j * DZ, DZ)], og_sem.at[q, j]
        )

    w_copy = pltpu.make_async_copy(w_ref, wall.at[z, xl], w_sem)
    saved_copy = pltpu.make_async_copy(saved_hbm, saved_ref, saved_sem)
    for q in range(NQ):
        for col in range(2):
            og_copy(q, col).start()
        if q == 1:
            w_copy.start()
    saved_copy.start()
    expert_row = lax.broadcasted_iota(jnp.int32, (EXPERTS, TOK), 0)
    weight_rows = weights_ref[...].astype(F32)
    hits = jnp.zeros((EXPERTS, TOK), F32)
    gates = jnp.zeros((EXPERTS, TOK), F32)
    for k in range(4):
        eq = expert_row == ids_ref[k : k + 1, :]
        hits = hits + jnp.where(eq, 1.0, 0.0)
        gates = gates + jnp.where(eq, weight_rows[k : k + 1, :], 0.0)
    earlier = (
        lax.broadcasted_iota(jnp.int32, (TOK, TOK), 0) < lax.broadcasted_iota(jnp.int32, (TOK, TOK), 1)
    )
    before = jnp.dot(
        hits.astype(BF16), jnp.where(earlier, 1.0, 0.0).astype(BF16), preferred_element_type=F32
    )
    meta_low[ex, 0:EXPERTS, :] = jnp.where(hits > 0.5, before, -1.0).astype(BF16)
    meta_low[ex, EXPERTS : 2 * EXPERTS, :] = gates.astype(BF16)

    pl.semaphore_wait(barrier, EXPERTS + 2)


    ym8, yp8 = around_y(-1) * 2 + xh, around_y(1) * 2 + xh
    y2 = around_y(2) * 2 + xh
    flip = 1 - 2 * xh
    lower, upper = pl.ds(0, TOK // 2), pl.ds(TOK // 2, TOK // 2)

    def a_copy(kind, q, src8, rows, to):
        ref = tok.at[src8, q] if rows is None else tok.at[src8, q, rows]
        return remote(ref, ref, a_send.at[kind, q], a_recv.at[kind, q], to)

    def a_out(kind, q):
        return (
            lambda: a_copy(0, q, me8, None, h_mate),
            lambda: a_copy(1, q, me8, None, at_y(1)),
            lambda: a_copy(2, q, me8, None, at_y(-1)),
            lambda: a_copy(3, q, me8 + flip, None, at_y(1)),
            lambda: a_copy(4, q, me8 + flip, None, at_y(-1)),
            lambda: a_copy(5, q, ym8, lower, at_y(1)),
            lambda: a_copy(6, q, yp8, upper, at_y(-1)),
            lambda: a_copy(7, q, ym8 + flip, lower, at_y(1)),
            lambda: a_copy(8, q, yp8 + flip, upper, at_y(-1)),
        )[kind]()

    def a_in(kind, q):
        return (
            lambda: a_copy(0, q, me8 + flip, None, h_mate),
            lambda: a_copy(1, q, ym8, None, at_y(1)),
            lambda: a_copy(2, q, yp8, None, at_y(-1)),
            lambda: a_copy(3, q, ym8 + flip, None, at_y(1)),
            lambda: a_copy(4, q, yp8 + flip, None, at_y(-1)),
            lambda: a_copy(5, q, y2, lower, at_y(1)),
            lambda: a_copy(6, q, y2, upper, at_y(-1)),
            lambda: a_copy(7, q, y2 + flip, lower, at_y(1)),
            lambda: a_copy(8, q, y2 + flip, upper, at_y(-1)),
        )[kind]()

    def a_own(q):
        for kind in (1, 2):
            a_out(kind, q).start()

    half = DZ // 2

    def bz_copy(way, step, h, to_send):
        sign = 1 if way == 0 else -1
        dist = step - 1 if to_send else step
        ref = wall.at[around_z(-sign * dist), xl, pl.ds(h * half, half)]
        sems = (way, step - 1, h)
        return remote(ref, ref, bz_send.at[sems], bz_recv.at[sems], at_z(sign))

    def bz_next(step, h, ways=(0, 1)):
        for way in ways:
            bz_copy(way, step, h, False).wait_recv()
            if step < 3 or (step == 3 and h == way):
                bz_copy(way, step + 1, h, True).start()

    def bx_copy(i, mine):
        ref = wall.at[around_z(i), xl if mine else 1 - xl]
        if i in (1, 7):
            ref = ref.at[pl.ds(half, half)]
        return remote(ref, ref, bx_send.at[i], bx_recv.at[i], x_mate)

    def bn_copy(way, to_send):
        sign = 1 if way == 0 else -1
        ref = wall.at[around_z(0 if to_send else -sign), 1 - xl, pl.ds(0, half)]
        return remote(ref, ref, bn_send.at[way], bn_recv.at[way], at_z(sign))

    w_copy.wait()
    for h in range(2):
        for way in range(2):
            bz_copy(way, 1, h, True).start()

    def m_copy(i, slot, to):
        return remote(meta_low.at[slot], meta_low.at[slot], m_send.at[i], m_recv.at[i], {"expert": to})

    def meta_send(i, carry):
        m_copy(i, ex, lax.rem(ex + i, EXPERTS)).start()
        return carry

    lax.fori_loop(1, EXPERTS, meta_send, 0)

    for q in range(NQ):
        for j in range(2):
            og_copy(q, j).wait()
        a_out(0, q).start()
        if q < 2:
            a_own(q)
        if q == 2:
            bx_copy(0, True).start()

    def factors(s, carry):
        row = lax.rem(s, 2) * 8 + s // 2
        for part in range(2):
            lanes = pl.ds(part * (FF // 2), FF // 2)
            g = saved_ref[s, :, part * (FF // 2) : (part + 1) * (FF // 2)].astype(F32)
            u = saved_ref[s, :, FF + part * (FF // 2) : FF + (part + 1) * (FF // 2)].astype(F32)
            sig = jax.nn.sigmoid(g)
            silu = g * sig
            act_low[row, :, lanes] = (silu * u).astype(BF16)
            fac_g[row, :, lanes] = u * sig * (1.0 + g * (1.0 - sig))
            fac_u[row, :, lanes] = silu
        return carry

    saved_copy.wait()
    lax.fori_loop(0, 4, factors, 0)

    def meta_wait(i, carry):
        m_copy(i, lax.rem(ex - i + EXPERTS, EXPERTS), ex).wait_recv()
        return carry

    cap_row = lax.broadcasted_iota(jnp.int32, (CAP, TOK), 0).astype(F32)

    def choose(s, carry):
        hit = cap_row == meta[s, pl.ds(ex, 1), :]
        value = jnp.where(hit, meta[s, pl.ds(EXPERTS + ex, 1), :], 0.0)
        row = lax.rem(s, 2) * 8 + s // 2
        gate[row] = jnp.broadcast_to(jnp.sum(value, axis=1, keepdims=True), (CAP, TOK))
        return carry


    def choose_both(s8, carry):
        s = s8 * 2 + core
        mate_ex = (y * 2 + xh) * 2 + (1 - core)
        mine = cap_row == meta[s, pl.ds(ex, 1), :]
        its = cap_row == meta[s, pl.ds(mate_ex, 1), :]
        sel[s8, 0:CAP, :] = jnp.where(mine, 1.0, 0.0).astype(BF16)
        sel[s8, CAP : 2 * CAP, :] = jnp.where(its, 1.0, 0.0).astype(BF16)
        return carry

    def choose_rows():
        lax.fori_loop(1, EXPERTS, meta_wait, 0)
        meta[...] = meta_low[...].astype(F32)
        lax.fori_loop(0, 16, choose, 0)
        lax.fori_loop(0, 8, choose_both, 0)

    def s_copy(q, mine):
        c = core if mine else 1 - core
        return remote(stage.at[q], routed.at[q, c], s_send.at[q], s_recv.at[q], c_mate)

    def select(q):
        def one(s8, carry):
            got = jnp.dot(sel[s8], tok[s8, q], preferred_element_type=F32).astype(BF16)
            routed[q, core, s8] = got[0:CAP]
            stage[q, s8] = got[CAP : 2 * CAP]
            return carry

        lax.fori_loop(0, 8, one, 0)
        s_copy(q, True).start()

    def partial_sum(q, j):
        rows = routed[q, :, :, :, j * DZ : (j + 1) * DZ].reshape(16 * CAP, DZ).astype(F32)
        scale = gate[...].reshape(16 * CAP, TOK)[:, 0:1]
        weighted = (rows * scale).astype(BF16)
        part[j] = lax.dot_general(
            weighted,
            act_low[...].reshape(16 * CAP, FF),
            (((0,), (0,)), ((), ())),
            preferred_element_type=F32,
        )

    def c_half(way, order):
        return remote(
            rs_half.at[way, order],
            rs_half_in.at[way, order],
            c_send.at[way, 0, order],
            c_recv.at[way, 0, order],
            at_z(1 - 2 * way),
        )

    def c_full(way, hop, order):
        return remote(
            rs_out.at[way, hop - 1, order],
            rs_in.at[way, hop - 1, order],
            c_send.at[way, hop, order],
            c_recv.at[way, hop, order],
            at_z(1 - 2 * way),
        )

    def reduce(q):
        for j in range(2):
            partial_sum(q, j)
            if q == 0:
                for way in range(2):
                    rs_half[way, j] = part[j, way * half : (way + 1) * half, :].astype(BF16)
                    c_half(way, j).start()

    def chain(q):
        order, hop = (q - 1) % 2, (q + 1) // 2
        for way in range(2):
            if hop == 1:
                c_half(way, order).wait_recv()
                mid = slice(way * half, (way + 1) * half)
                rest = slice((1 - way) * half, (2 - way) * half)
                rs_out[way, 0, order, mid] = (
                    part[way, mid, :] + rs_half_in[way, order].astype(F32)
                ).astype(BF16)
                rs_out[way, 0, order, rest] = part[way, rest, :].astype(BF16)
            else:
                c_full(way, hop - 1, order).wait_recv()
                rs_out[way, hop - 1, order] = (
                    part[way] + rs_in[way, hop - 2, order].astype(F32)
                ).astype(BF16)
            c_full(way, hop, order).start()

    def f_copy():
        return remote(fin_out, fin_in, f_send, f_recv, x_mate)

    def back(q):
        for c in range(2):
            rows = slice(c * 8 * CAP, (c + 1) * 8 * CAP)
            got = acc[rows, :]
            for j in range(2):
                dist, order = PIECES[q][j]
                got = got + jnp.dot(
                    routed[q, c, :, :, j * DZ : (j + 1) * DZ].reshape(8 * CAP, DZ),
                    wall[around_z(dist), column(order)],
                    preferred_element_type=F32,
                )
            acc[rows, :] = got

    acc[...] = jnp.zeros_like(acc)

    for t in range(NQ + 2):
        if 1 <= t - 3 < NQ - 1:
            chain(t - 3)
        if t < NQ:
            a_in(0, t).wait_recv()
            a_out(3, t).start()
            a_out(4, t).start()
            a_in(1, t).wait_recv()
            a_out(5, t).start()
            a_in(2, t).wait_recv()
            a_out(6, t).start()
        for q in (t + 2,):
            if q < NQ:
                a_own(q)
        if 0 <= t - 1 < NQ:
            a_in(3, t - 1).wait_recv()
            a_out(7, t - 1).start()
            a_in(4, t - 1).wait_recv()
            a_out(8, t - 1).start()
        if t == 0:
            bz_next(1, 0)
        if t == 1:
            bz_next(1, 1)
        if t == 2:
            bz_next(2, 0)
            bx_copy(0, False).wait_recv()
            bn_copy(0, True).start()
            bn_copy(1, True).start()
        if t == 3:
            bz_next(3, 0)
        if t == 4:
            bz_next(3, 1)
        if t == 6:
            bz_copy(0, 4, 0, False).wait_recv()
            bz_copy(1, 4, 1, False).wait_recv()
        for i in {1: (1, 7), 4: (3, 5), 6: (4,)}.get(t, ()):
            bx_copy(i, True).start()
        if t < 2:
            lax.fori_loop(4 + 6 * t, 10 + 6 * t, factors, 0)
        if t == 1:
            choose_rows()
        if t == 7:
            for i in (1, 7, 2, 6):
                bx_copy(i, False).wait_recv()
            bn_copy(0, False).wait_recv()
            bn_copy(1, False).wait_recv()
        if 0 <= t - 2 < NQ:
            for kind in (5, 6, 7, 8):
                a_in(kind, t - 2).wait_recv()
            select(t - 2)
            if t == 2:
                bz_next(2, 1)
                bx_copy(2, True).start()
                bx_copy(6, True).start()
            if t == 7:
                back(3)
            if t == 8:
                back(4)
                back(5)
            s_copy(t - 2, False).wait_recv()
            reduce(t - 2)

    def g_copy(i, src, dst, to):
        return remote(sc_out.at[src], sc_in.at[dst], g_send.at[i], g_recv.at[i], {"expert": to})

    def finish(c):
        def one(s8, carry):
            s = s8 * 2 + c
            row = c * 8 + s8
            out = acc[pl.ds(pl.multiple_of(row * CAP, CAP), CAP), :]
            scale = gate[row][:, 0:1]
            grad = out * scale
            silu = fac_u[row]
            u = saved_ref[s, :, FF : 2 * FF].astype(F32)
            pre_ref[s, :, 0:FF] = (grad * fac_g[row]).astype(BF16)
            pre_ref[s, :, FF : 2 * FF] = (grad * silu).astype(BF16)
            score = jnp.sum(out * (silu * u), axis=1, keepdims=True)
            sc_out[s] = jnp.broadcast_to(score, (CAP, TOK))
            return carry

        lax.fori_loop(0, 8, one, 0)

    def last(order):
        c_full(0, 3, order).wait_recv()
        c_full(1, 3, order).wait_recv()
        return part[order] + rs_in[0, 2, order].astype(F32) + rs_in[1, 2, order].astype(F32)

    back(6)
    back(7)
    bx_copy(3, False).wait_recv()
    bx_copy(5, False).wait_recv()
    back(1)
    back(2)
    def drain_meta(i, carry):
        m_copy(i, ex, lax.rem(ex + i, EXPERTS)).wait_send()
        return carry

    lax.fori_loop(1, EXPERTS, drain_meta, 0)
    for q in range(NQ):
        for kind in range(9):
            a_out(kind, q).wait_send()
        s_copy(q, True).wait_send()
        bx_copy(q, True).wait_send()
    for way in range(2):
        for step in range(1, 5):
            for h in range(2):
                if step < 4 or h == way:
                    bz_copy(way, step, h, True).wait_send()
        bn_copy(way, True).wait_send()
        for order in range(2):
            c_half(way, order).wait_send()
            for hop in range(1, 4):
                if hop < 3:
                    c_full(way, hop, order).wait_send()
    fin_out[...] = last(0).astype(BF16)
    f_copy().start()
    bx_copy(4, False).wait_recv()
    back(0)

    def pre_copy(c, s8):
        ref = s8 * 2 + c
        return pltpu.make_async_copy(pre_ref.at[ref], pre_hbm.at[ref], pre_sem.at[ref])

    def pre_out(c):
        for s8 in range(8):
            pre_copy(c, s8).start()

    finish(0)
    pre_out(0)
    finish(1)
    pre_out(1)

    def score_send(i, carry):
        to = lax.rem(ex + i, EXPERTS)
        g_copy(i, to, ex, to).start()
        return carry

    lax.fori_loop(1, EXPERTS, score_send, 0)
    sc_in[ex] = sc_out[ex]

    own = last(1)
    f_copy().wait_recv()
    down_ref[...] = (own + fin_in[...].astype(F32)).astype(BF16)

    def score_wait(i, carry):
        g_copy(i, ex, lax.rem(ex - i + EXPERTS, EXPERTS), ex).wait_recv()
        return carry

    lax.fori_loop(1, EXPERTS, score_wait, 0)

    rows = [jnp.zeros((1, TOK), F32) for _ in range(4)]
    for e in range(EXPERTS):
        hit = cap_row == meta[ex, e : e + 1, :]
        value = jnp.sum(jnp.where(hit, sc_in[e], 0.0), axis=0, keepdims=True)
        for k in range(4):
            rows[k] = rows[k] + jnp.where(ids_ref[k : k + 1, :] == e, value, 0.0)
    for k in range(4):
        gate_ref[k : k + 1, :] = rows[k]

    def drain_scores(i, carry):
        to = lax.rem(ex + i, EXPERTS)
        g_copy(i, to, ex, to).wait_send()
        return carry

    lax.fori_loop(1, EXPERTS, drain_scores, 0)
    f_copy().wait_send()
    for way in range(2):
        for order in range(2):
            c_full(way, 3, order).wait_send()
    for q in range(NQ):
        for c in range(2):
            pre_copy(c, q).wait()


def shards(out_grad, expert_ids, gate_weights, saved_acts, down_weight):
    vmem = pl.BlockSpec(memory_space=pltpu.VMEM)
    hbm = pl.BlockSpec(memory_space=pl.ANY)
    dma = pltpu.SemaphoreType.DMA
    pre, down, gate_t = pl.pallas_call(
        kernel,
        out_shape=(
            jax.ShapeDtypeStruct((EXPERTS, CAP, 2 * FF), BF16),
            jax.ShapeDtypeStruct((DZ, FF), BF16),
            jax.ShapeDtypeStruct((4, TOK), F32),
        ),
        in_specs=[hbm, vmem, vmem, hbm, hbm],
        out_specs=(hbm, vmem, vmem),
        scratch_shapes=[
            pltpu.VMEM((EXPERTS, CAP, 2 * FF), BF16),
            pltpu.VMEM((EXPERTS, CAP, 2 * FF), BF16),
            pltpu.VMEM((8, NQ, TOK, 2 * DZ), BF16),
            pltpu.VMEM((NQ, 2, 8, CAP, 2 * DZ), BF16),
            pltpu.VMEM((NQ, 8, CAP, 2 * DZ), BF16),
            pltpu.VMEM((8, 2 * CAP, TOK), BF16),
            pltpu.VMEM((16, CAP, TOK), F32),
            pltpu.VMEM((16, 2 * EXPERTS, TOK), BF16),
            pltpu.VMEM((16, 2 * EXPERTS, TOK), F32),
            pltpu.VMEM((NZ, 2, DZ, FF), BF16),
            pltpu.VMEM((16, CAP, FF), BF16),
            pltpu.VMEM((16, CAP, FF), F32),
            pltpu.VMEM((16, CAP, FF), F32),
            pltpu.VMEM((16 * CAP, FF), F32),
            pltpu.VMEM((2, 2, DZ // 2, FF), BF16),
            pltpu.VMEM((2, 3, 2, DZ, FF), BF16),
            pltpu.VMEM((2, 2, DZ // 2, FF), BF16),
            pltpu.VMEM((2, 3, 2, DZ, FF), BF16),
            pltpu.VMEM((DZ, FF), BF16),
            pltpu.VMEM((DZ, FF), BF16),
            pltpu.VMEM((2, DZ, FF), F32),
            pltpu.VMEM((16, CAP, TOK), F32),
            pltpu.VMEM((16, CAP, TOK), F32),
            dma((9, NQ)), dma((9, NQ)),
            dma((NQ,)), dma((NQ,)),
            dma((EXPERTS,)), dma((EXPERTS,)),
            dma((2, 4, 2)), dma((2, 4, 2)),
            dma((NZ,)), dma((NZ,)),
            dma((2,)), dma((2,)),
            dma((2, 4, 2)), dma((2, 4, 2)),
            dma(()), dma(()),
            dma((EXPERTS,)), dma((EXPERTS,)),
            dma((NQ, 2)), dma(()), dma(()), dma((EXPERTS,)),
        ],
        compiler_params=pltpu.CompilerParams(
            collective_id=0, has_side_effects=True, vmem_limit_bytes=60 * 1024 * 1024
        ),
    )(out_grad, expert_ids.T, gate_weights.T, saved_acts[0, :, 0], down_weight[0])
    return pre[None, :, None], down[None], gate_t.T


def solution(mesh):
    placed = (
        P(("dp", "expert"), None),
        P(("dp", "expert"), None),
        P(("dp", "expert"), None),
        P("dp", None, "expert", None, None),
        P("expert", "dp", None),
    )
    return jax.shard_map(
        shards,
        mesh=mesh,
        in_specs=placed,
        out_specs=(
            P("dp", None, "expert", None, None),
            P("expert", "dp", None),
            P(("dp", "expert"), None),
        ),
        check_vma=False,
    )
```

```python
import jax
import jax.numpy as jnp
from jax import lax
from jax.experimental import pallas as pl
from jax.experimental.pallas import tpu as pltpu
from jax.sharding import PartitionSpec as P

MESH = pl.DeviceIdType.MESH
F32 = jnp.float32
BF16 = jnp.bfloat16

EXPERTS = 16
CAP = 48
TOK = 128
FF = 768
DZ = 256
NQ = 8
NZ = 8
NY = 4
PIECES = (
    ((4, 0), (4, 1)),
    ((3, 0), (-3, 0)),
    ((3, 1), (-3, 1)),
    ((2, 0), (-2, 0)),
    ((2, 1), (-2, 1)),
    ((1, 0), (-1, 0)),
    ((1, 1), (-1, 1)),
    ((0, 0), (0, 1)),
)


def kernel(
    og_ref, ids_ref, weights_ref, saved_hbm, w_ref,
    pre_hbm, down_ref, gate_ref,
    saved_ref, pre_ref, tok, routed, stage, sel, gate, meta_low, meta, wall, act_low, fac_g, fac_u, acc,
    rs_half, rs_out, rs_half_in, rs_in, fin_out, fin_in, part, sc_out, sc_in,
    a_send, a_recv, s_send, s_recv, m_send, m_recv,
    bz_send, bz_recv, bx_send, bx_recv, bn_send, bn_recv, c_send, c_recv, l_send, l_recv, f_send, f_recv,
    g_send, g_recv, og_sem, w_sem, saved_sem, pre_sem,
):
    dp = lax.axis_index("dp")
    ex = lax.axis_index("expert")
    xl, z = dp // NZ, lax.rem(dp, NZ)
    y, xh, core = ex // 4, lax.rem(ex // 2, 2), lax.rem(ex, 2)

    def around_z(d):
        return lax.rem(z + (d + NZ), NZ)

    def around_y(d):
        return lax.rem(y + (d + NY), NY)

    def at_z(d):
        return {"dp": xl * NZ + around_z(d)}

    def at_y(d):
        return {"expert": (around_y(d) * 2 + xh) * 2 + core}

    x_mate = {"dp": (1 - xl) * NZ + z}
    h_mate = {"expert": (y * 2 + (1 - xh)) * 2 + core}
    c_mate = {"expert": (y * 2 + xh) * 2 + (1 - core)}

    def remote(src, dst, send, recv, to):
        return pltpu.make_async_remote_copy(
            src_ref=src, dst_ref=dst, send_sem=send, recv_sem=recv, device_id=to, device_id_type=MESH
        )

    barrier = pltpu.get_barrier_semaphore()

    def greet(i, carry):
        pl.semaphore_signal(
            barrier, inc=1, device_id={"expert": lax.rem(ex + i, EXPERTS)}, device_id_type=MESH
        )
        return carry

    lax.fori_loop(1, EXPERTS, greet, 0)
    for to in (x_mate, at_z(1), at_z(-1)):
        pl.semaphore_signal(barrier, inc=1, device_id=to, device_id_type=MESH)

    me8 = y * 2 + xh

    def column(order):
        return 1 - xl if order == 0 else xl

    def og_copy(q, j):
        dist, order = PIECES[q][j]
        cols = pl.ds(pl.multiple_of((column(order) * NZ + around_z(dist)) * DZ, DZ), DZ)
        return pltpu.make_async_copy(
            og_ref.at[:, cols], tok.at[me8, q, :, pl.ds(j * DZ, DZ)], og_sem.at[q, j]
        )

    w_copy = pltpu.make_async_copy(w_ref, wall.at[z, xl], w_sem)
    saved_copy = pltpu.make_async_copy(saved_hbm, saved_ref, saved_sem)
    for q in range(NQ):
        for col in range(2):
            og_copy(q, col).start()
        if q == 1:
            w_copy.start()
    saved_copy.start()
    expert_row = lax.broadcasted_iota(jnp.int32, (EXPERTS, TOK), 0)
    weight_rows = weights_ref[...].astype(F32)
    hits = jnp.zeros((EXPERTS, TOK), F32)
    gates = jnp.zeros((EXPERTS, TOK), F32)
    for k in range(4):
        eq = expert_row == ids_ref[k : k + 1, :]
        hits = hits + jnp.where(eq, 1.0, 0.0)
        gates = gates + jnp.where(eq, weight_rows[k : k + 1, :], 0.0)
    earlier = (
        lax.broadcasted_iota(jnp.int32, (TOK, TOK), 0) < lax.broadcasted_iota(jnp.int32, (TOK, TOK), 1)
    )
    before = jnp.dot(
        hits.astype(BF16), jnp.where(earlier, 1.0, 0.0).astype(BF16), preferred_element_type=F32
    )
    meta_low[ex, 0:EXPERTS, :] = jnp.where(hits > 0.5, before, -1.0).astype(BF16)
    meta_low[ex, EXPERTS : 2 * EXPERTS, :] = gates.astype(BF16)

    pl.semaphore_wait(barrier, EXPERTS + 2)


    ym8, yp8 = around_y(-1) * 2 + xh, around_y(1) * 2 + xh
    y2 = around_y(2) * 2 + xh
    flip = 1 - 2 * xh
    lower, upper = pl.ds(0, TOK // 2), pl.ds(TOK // 2, TOK // 2)

    def a_copy(kind, q, src8, rows, to):
        ref = tok.at[src8, q] if rows is None else tok.at[src8, q, rows]
        return remote(ref, ref, a_send.at[kind, q], a_recv.at[kind, q], to)

    def a_out(kind, q):
        return (
            lambda: a_copy(0, q, me8, None, h_mate),
            lambda: a_copy(1, q, me8, None, at_y(1)),
            lambda: a_copy(2, q, me8, None, at_y(-1)),
            lambda: a_copy(3, q, me8 + flip, None, at_y(1)),
            lambda: a_copy(4, q, me8 + flip, None, at_y(-1)),
            lambda: a_copy(5, q, ym8, lower, at_y(1)),
            lambda: a_copy(6, q, yp8, upper, at_y(-1)),
            lambda: a_copy(7, q, ym8 + flip, lower, at_y(1)),
            lambda: a_copy(8, q, yp8 + flip, upper, at_y(-1)),
        )[kind]()

    def a_in(kind, q):
        return (
            lambda: a_copy(0, q, me8 + flip, None, h_mate),
            lambda: a_copy(1, q, ym8, None, at_y(1)),
            lambda: a_copy(2, q, yp8, None, at_y(-1)),
            lambda: a_copy(3, q, ym8 + flip, None, at_y(1)),
            lambda: a_copy(4, q, yp8 + flip, None, at_y(-1)),
            lambda: a_copy(5, q, y2, lower, at_y(1)),
            lambda: a_copy(6, q, y2, upper, at_y(-1)),
            lambda: a_copy(7, q, y2 + flip, lower, at_y(1)),
            lambda: a_copy(8, q, y2 + flip, upper, at_y(-1)),
        )[kind]()

    def a_own(q):
        for kind in (1, 2):
            a_out(kind, q).start()

    half = DZ // 2

    def bz_copy(way, step, h, to_send):
        sign = 1 if way == 0 else -1
        dist = step - 1 if to_send else step
        ref = wall.at[around_z(-sign * dist), xl, pl.ds(h * half, half)]
        sems = (way, step - 1, h)
        return remote(ref, ref, bz_send.at[sems], bz_recv.at[sems], at_z(sign))

    def bz_next(step, h, ways=(0, 1)):
        for way in ways:
            bz_copy(way, step, h, False).wait_recv()
            if step < 3 or (step == 3 and h == way):
                bz_copy(way, step + 1, h, True).start()

    def bx_copy(i, mine):
        ref = wall.at[around_z(i), xl if mine else 1 - xl]
        if i in (1, 7):
            ref = ref.at[pl.ds(half, half)]
        return remote(ref, ref, bx_send.at[i], bx_recv.at[i], x_mate)

    def bn_copy(way, to_send):
        sign = 1 if way == 0 else -1
        ref = wall.at[around_z(0 if to_send else -sign), 1 - xl, pl.ds(0, half)]
        return remote(ref, ref, bn_send.at[way], bn_recv.at[way], at_z(sign))

    w_copy.wait()
    for h in range(2):
        for way in range(2):
            bz_copy(way, 1, h, True).start()

    def m_copy(i, slot, to):
        return remote(meta_low.at[slot], meta_low.at[slot], m_send.at[i], m_recv.at[i], {"expert": to})

    def meta_send(i, carry):
        m_copy(i, ex, lax.rem(ex + i, EXPERTS)).start()
        return carry

    lax.fori_loop(1, EXPERTS, meta_send, 0)

    for q in range(NQ):
        for j in range(2):
            og_copy(q, j).wait()
        a_out(0, q).start()
        if q < 2:
            a_own(q)
        if q == 2:
            bx_copy(0, True).start()

    def factors(s, carry):
        row = lax.rem(s, 2) * 8 + s // 2
        for part in range(2):
            lanes = pl.ds(part * (FF // 2), FF // 2)
            g = saved_ref[s, :, part * (FF // 2) : (part + 1) * (FF // 2)].astype(F32)
            u = saved_ref[s, :, FF + part * (FF // 2) : FF + (part + 1) * (FF // 2)].astype(F32)
            sig = jax.nn.sigmoid(g)
            silu = g * sig
            act_low[row, :, lanes] = (silu * u).astype(BF16)
            fac_g[row, :, lanes] = u * sig * (1.0 + g * (1.0 - sig))
            fac_u[row, :, lanes] = silu
        return carry

    saved_copy.wait()
    lax.fori_loop(0, 4, factors, 0)

    def meta_wait(i, carry):
        m_copy(i, lax.rem(ex - i + EXPERTS, EXPERTS), ex).wait_recv()
        return carry

    cap_row = lax.broadcasted_iota(jnp.int32, (CAP, TOK), 0).astype(F32)

    def choose(s, carry):
        hit = cap_row == meta[s, pl.ds(ex, 1), :]
        value = jnp.where(hit, meta[s, pl.ds(EXPERTS + ex, 1), :], 0.0)
        row = lax.rem(s, 2) * 8 + s // 2
        gate[row] = jnp.broadcast_to(jnp.sum(value, axis=1, keepdims=True), (CAP, TOK))
        return carry


    def choose_both(s8, carry):
        s = s8 * 2 + core
        mate_ex = (y * 2 + xh) * 2 + (1 - core)
        mine = cap_row == meta[s, pl.ds(ex, 1), :]
        its = cap_row == meta[s, pl.ds(mate_ex, 1), :]
        sel[s8, 0:CAP, :] = jnp.where(mine, 1.0, 0.0).astype(BF16)
        sel[s8, CAP : 2 * CAP, :] = jnp.where(its, 1.0, 0.0).astype(BF16)
        return carry

    def choose_rows():
        lax.fori_loop(1, EXPERTS, meta_wait, 0)
        meta[...] = meta_low[...].astype(F32)
        lax.fori_loop(0, 16, choose, 0)
        lax.fori_loop(0, 8, choose_both, 0)

    def s_copy(q, mine):
        c = core if mine else 1 - core
        return remote(stage.at[q], routed.at[q, c], s_send.at[q], s_recv.at[q], c_mate)

    def select(q):
        def one(s8, carry):
            got = jnp.dot(sel[s8], tok[s8, q], preferred_element_type=F32).astype(BF16)
            routed[q, core, s8] = got[0:CAP]
            stage[q, s8] = got[CAP : 2 * CAP]
            return carry

        lax.fori_loop(0, 8, one, 0)
        s_copy(q, True).start()

    def partial_sum(q, j):
        rows = routed[q, :, :, :, j * DZ : (j + 1) * DZ].reshape(16 * CAP, DZ).astype(F32)
        scale = gate[...].reshape(16 * CAP, TOK)[:, 0:1]
        weighted = (rows * scale).astype(BF16)
        part[j] = lax.dot_general(
            weighted,
            act_low[...].reshape(16 * CAP, FF),
            (((0,), (0,)), ((), ())),
            preferred_element_type=F32,
        )

    def c_half(way, order):
        return remote(
            rs_half.at[way, order],
            rs_half_in.at[way, order],
            c_send.at[way, 0, order],
            c_recv.at[way, 0, order],
            at_z(1 - 2 * way),
        )

    def c_full(way, hop, order):
        return remote(
            rs_out.at[way, hop - 1, order],
            rs_in.at[way, hop - 1, order],
            c_send.at[way, hop, order],
            c_recv.at[way, hop, order],
            at_z(1 - 2 * way),
        )

    def c_last(way, h):
        rows = pl.ds(h * half, half)
        return remote(
            rs_out.at[way, 2, 0, rows],
            rs_in.at[way, 2, 0, rows],
            l_send.at[way, h],
            l_recv.at[way, h],
            at_z(1 - 2 * way),
        )

    def reduce(q):
        for j in range(2):
            partial_sum(q, j)
            if q == 0:
                for way in range(2):
                    rs_half[way, j] = part[j, way * half : (way + 1) * half, :].astype(BF16)
                    c_half(way, j).start()

    def chain(q):
        order, hop = (q - 1) % 2, (q + 1) // 2
        for way in range(2):
            if hop == 1:
                c_half(way, order).wait_recv()
                mid = slice(way * half, (way + 1) * half)
                rest = slice((1 - way) * half, (2 - way) * half)
                rs_out[way, 0, order, mid] = (
                    part[way, mid, :] + rs_half_in[way, order].astype(F32)
                ).astype(BF16)
                rs_out[way, 0, order, rest] = part[way, rest, :].astype(BF16)
            else:
                c_full(way, hop - 1, order).wait_recv()
                rs_out[way, hop - 1, order] = (
                    part[way] + rs_in[way, hop - 2, order].astype(F32)
                ).astype(BF16)
            if (hop, order) == (3, 0):
                c_last(way, 0).start()
                c_last(way, 1).start()
            else:
                c_full(way, hop, order).start()

    def f_copy(h):
        rows = pl.ds(h * half, half)
        return remote(fin_out.at[rows], fin_in.at[rows], f_send.at[h], f_recv.at[h], x_mate)

    def back(q):
        for c in range(2):
            rows = slice(c * 8 * CAP, (c + 1) * 8 * CAP)
            got = acc[rows, :]
            for j in range(2):
                dist, order = PIECES[q][j]
                got = got + jnp.dot(
                    routed[q, c, :, :, j * DZ : (j + 1) * DZ].reshape(8 * CAP, DZ),
                    wall[around_z(dist), column(order)],
                    preferred_element_type=F32,
                )
            acc[rows, :] = got

    acc[...] = jnp.zeros_like(acc)

    for t in range(NQ + 2):
        if 1 <= t - 3 < NQ - 1:
            chain(t - 3)
        if t < NQ:
            a_in(0, t).wait_recv()
            a_out(3, t).start()
            a_out(4, t).start()
            a_in(1, t).wait_recv()
            a_out(5, t).start()
            a_in(2, t).wait_recv()
            a_out(6, t).start()
        for q in (t + 2,):
            if q < NQ:
                a_own(q)
        if 0 <= t - 1 < NQ:
            a_in(3, t - 1).wait_recv()
            a_out(7, t - 1).start()
            a_in(4, t - 1).wait_recv()
            a_out(8, t - 1).start()
        if t == 0:
            bz_next(1, 0)
        if t == 1:
            bz_next(1, 1)
        if t == 2:
            bz_next(2, 0)
            bx_copy(0, False).wait_recv()
            bn_copy(0, True).start()
            bn_copy(1, True).start()
        if t == 3:
            bz_next(3, 0)
        if t == 4:
            bz_next(3, 1)
        if t == 6:
            bz_copy(0, 4, 0, False).wait_recv()
            bz_copy(1, 4, 1, False).wait_recv()
        for i in {1: (1, 7), 4: (3, 5), 6: (4,)}.get(t, ()):
            bx_copy(i, True).start()
        if t < 2:
            lax.fori_loop(4 + 6 * t, 10 + 6 * t, factors, 0)
        if t == 1:
            choose_rows()
        if t == 7:
            for i in (1, 7, 2, 6):
                bx_copy(i, False).wait_recv()
            bn_copy(0, False).wait_recv()
            bn_copy(1, False).wait_recv()
        if 0 <= t - 2 < NQ:
            for kind in (5, 6, 7, 8):
                a_in(kind, t - 2).wait_recv()
            select(t - 2)
            if t == 2:
                bz_next(2, 1)
                bx_copy(2, True).start()
                bx_copy(6, True).start()
            if t == 7:
                back(3)
            if t == 8:
                back(4)
                back(5)
            s_copy(t - 2, False).wait_recv()
            reduce(t - 2)

    def g_copy(i, src, dst, to):
        return remote(sc_out.at[src], sc_in.at[dst], g_send.at[i], g_recv.at[i], {"expert": to})

    def finish(c):
        def one(s8, carry):
            s = s8 * 2 + c
            row = c * 8 + s8
            out = acc[pl.ds(pl.multiple_of(row * CAP, CAP), CAP), :]
            scale = gate[row][:, 0:1]
            grad = out * scale
            silu = fac_u[row]
            u = saved_ref[s, :, FF : 2 * FF].astype(F32)
            pre_ref[s, :, 0:FF] = (grad * fac_g[row]).astype(BF16)
            pre_ref[s, :, FF : 2 * FF] = (grad * silu).astype(BF16)
            score = jnp.sum(out * (silu * u), axis=1, keepdims=True)
            sc_out[s] = jnp.broadcast_to(score, (CAP, TOK))
            return carry

        lax.fori_loop(0, 8, one, 0)

    def last(order, rows):
        return (
            part[order, rows, :]
            + rs_in[0, 2, order, rows].astype(F32)
            + rs_in[1, 2, order, rows].astype(F32)
        )

    back(6)
    back(7)
    bx_copy(3, False).wait_recv()
    bx_copy(5, False).wait_recv()
    back(1)
    back(2)
    def drain_meta(i, carry):
        m_copy(i, ex, lax.rem(ex + i, EXPERTS)).wait_send()
        return carry

    lax.fori_loop(1, EXPERTS, drain_meta, 0)
    for q in range(NQ):
        for kind in range(9):
            a_out(kind, q).wait_send()
        s_copy(q, True).wait_send()
        bx_copy(q, True).wait_send()
    for way in range(2):
        for step in range(1, 5):
            for h in range(2):
                if step < 4 or h == way:
                    bz_copy(way, step, h, True).wait_send()
        bn_copy(way, True).wait_send()
        for order in range(2):
            c_half(way, order).wait_send()
            for hop in range(1, 4):
                if hop < 3:
                    c_full(way, hop, order).wait_send()
    for h in range(2):
        c_last(0, h).wait_recv()
        c_last(1, h).wait_recv()
        rows = slice(h * half, (h + 1) * half)
        fin_out[rows, :] = last(0, rows).astype(BF16)
        f_copy(h).start()
    bx_copy(4, False).wait_recv()
    back(0)

    def pre_copy(c, s8):
        ref = s8 * 2 + c
        return pltpu.make_async_copy(pre_ref.at[ref], pre_hbm.at[ref], pre_sem.at[ref])

    def pre_out(c):
        for s8 in range(8):
            pre_copy(c, s8).start()

    finish(0)
    pre_out(0)
    finish(1)
    pre_out(1)

    def score_send(i, carry):
        to = lax.rem(ex + i, EXPERTS)
        g_copy(i, to, ex, to).start()
        return carry

    lax.fori_loop(1, EXPERTS, score_send, 0)
    sc_in[ex] = sc_out[ex]

    c_full(0, 3, 1).wait_recv()
    c_full(1, 3, 1).wait_recv()
    for h in range(2):
        f_copy(h).wait_recv()
        rows = slice(h * half, (h + 1) * half)
        down_ref[rows, :] = (last(1, rows) + fin_in[rows, :].astype(F32)).astype(BF16)

    def score_wait(i, carry):
        g_copy(i, ex, lax.rem(ex - i + EXPERTS, EXPERTS), ex).wait_recv()
        return carry

    lax.fori_loop(1, EXPERTS, score_wait, 0)

    rows = [jnp.zeros((1, TOK), F32) for _ in range(4)]
    for e in range(EXPERTS):
        hit = cap_row == meta[ex, e : e + 1, :]
        value = jnp.sum(jnp.where(hit, sc_in[e], 0.0), axis=0, keepdims=True)
        for k in range(4):
            rows[k] = rows[k] + jnp.where(ids_ref[k : k + 1, :] == e, value, 0.0)
    for k in range(4):
        gate_ref[k : k + 1, :] = rows[k]

    def drain_scores(i, carry):
        to = lax.rem(ex + i, EXPERTS)
        g_copy(i, to, ex, to).wait_send()
        return carry

    lax.fori_loop(1, EXPERTS, drain_scores, 0)
    f_copy(0).wait_send()
    f_copy(1).wait_send()
    for way in range(2):
        c_full(way, 3, 1).wait_send()
        c_last(way, 0).wait_send()
        c_last(way, 1).wait_send()
    for q in range(NQ):
        for c in range(2):
            pre_copy(c, q).wait()


def shards(out_grad, expert_ids, gate_weights, saved_acts, down_weight):
    vmem = pl.BlockSpec(memory_space=pltpu.VMEM)
    hbm = pl.BlockSpec(memory_space=pl.ANY)
    dma = pltpu.SemaphoreType.DMA
    pre, down, gate_t = pl.pallas_call(
        kernel,
        out_shape=(
            jax.ShapeDtypeStruct((EXPERTS, CAP, 2 * FF), BF16),
            jax.ShapeDtypeStruct((DZ, FF), BF16),
            jax.ShapeDtypeStruct((4, TOK), F32),
        ),
        in_specs=[hbm, vmem, vmem, hbm, hbm],
        out_specs=(hbm, vmem, vmem),
        scratch_shapes=[
            pltpu.VMEM((EXPERTS, CAP, 2 * FF), BF16),
            pltpu.VMEM((EXPERTS, CAP, 2 * FF), BF16),
            pltpu.VMEM((8, NQ, TOK, 2 * DZ), BF16),
            pltpu.VMEM((NQ, 2, 8, CAP, 2 * DZ), BF16),
            pltpu.VMEM((NQ, 8, CAP, 2 * DZ), BF16),
            pltpu.VMEM((8, 2 * CAP, TOK), BF16),
            pltpu.VMEM((16, CAP, TOK), F32),
            pltpu.VMEM((16, 2 * EXPERTS, TOK), BF16),
            pltpu.VMEM((16, 2 * EXPERTS, TOK), F32),
            pltpu.VMEM((NZ, 2, DZ, FF), BF16),
            pltpu.VMEM((16, CAP, FF), BF16),
            pltpu.VMEM((16, CAP, FF), F32),
            pltpu.VMEM((16, CAP, FF), F32),
            pltpu.VMEM((16 * CAP, FF), F32),
            pltpu.VMEM((2, 2, DZ // 2, FF), BF16),
            pltpu.VMEM((2, 3, 2, DZ, FF), BF16),
            pltpu.VMEM((2, 2, DZ // 2, FF), BF16),
            pltpu.VMEM((2, 3, 2, DZ, FF), BF16),
            pltpu.VMEM((DZ, FF), BF16),
            pltpu.VMEM((DZ, FF), BF16),
            pltpu.VMEM((2, DZ, FF), F32),
            pltpu.VMEM((16, CAP, TOK), F32),
            pltpu.VMEM((16, CAP, TOK), F32),
            dma((9, NQ)), dma((9, NQ)),
            dma((NQ,)), dma((NQ,)),
            dma((EXPERTS,)), dma((EXPERTS,)),
            dma((2, 4, 2)), dma((2, 4, 2)),
            dma((NZ,)), dma((NZ,)),
            dma((2,)), dma((2,)),
            dma((2, 4, 2)), dma((2, 4, 2)),
            dma((2, 2)), dma((2, 2)),
            dma((2,)), dma((2,)),
            dma((EXPERTS,)), dma((EXPERTS,)),
            dma((NQ, 2)), dma(()), dma(()), dma((EXPERTS,)),
        ],
        compiler_params=pltpu.CompilerParams(
            collective_id=0, has_side_effects=True, vmem_limit_bytes=60 * 1024 * 1024
        ),
    )(out_grad, expert_ids.T, gate_weights.T, saved_acts[0, :, 0], down_weight[0])
    return pre[None, :, None], down[None], gate_t.T


def solution(mesh):
    placed = (
        P(("dp", "expert"), None),
        P(("dp", "expert"), None),
        P(("dp", "expert"), None),
        P("dp", None, "expert", None, None),
        P("expert", "dp", None),
    )
    return jax.shard_map(
        shards,
        mesh=mesh,
        in_specs=placed,
        out_specs=(
            P("dp", None, "expert", None, None),
            P("expert", "dp", None),
            P(("dp", "expert"), None),
        ),
        check_vma=False,
    )
```
